32 devices in a mesh: fsdp: 8 (over z, y), ctx: 4 (over x, core).
Axes of the slice: x: 2, y: 2, z: 4, core: 2. Of those that a mesh axis runs over, the one named last changes fastest.
Arguments:
- hidden_in: bfloat16 [16, 1024, 1024], P('fsdp', 'ctx'), may hold values from -6 to 6
- segment_ids: int32 [16, 1024], P('fsdp'), may hold values from 0 to 3, never falling along the last dimension, each value on 1 to 768 neighbouring positions
- joint_weight: bfloat16 [1024, 3072], P('fsdp'), may hold values from -0.1875 to 0.1875
- joint_bias: bfloat16 [2048], P('fsdp'), may hold values from -3 to 3
- mixer_weight: bfloat16 [1024, 1024], P('fsdp'), may hold values from -1 to 1
- mixer_bias: bfloat16 [1024], P('fsdp'), may hold values from -3 to 3
- first_gain: bfloat16 [1024], P('fsdp'), may hold values from 0.5 to 1.5
- first_shift: bfloat16 [1024], P('fsdp'), may hold values from -3 to 3
- expand_weight: bfloat16 [1024, 4096], P('fsdp'), may hold values from -0.1875 to 0.1875
- expand_bias: bfloat16 [4096], P('fsdp'), may hold values from -3 to 3
- shrink_weight: bfloat16 [4096, 1024], P('fsdp'), may hold values from -0.09375 to 0.09375
- shrink_bias: bfloat16 [1024], P('fsdp'), may hold values from -3 to 3
- second_gain: bfloat16 [1024], P('fsdp'), may hold values from 0.5 to 1.5
- second_shift: bfloat16 [1024], P('fsdp'), may hold values from -3 to 3
- output_cotangent: bfloat16 [16, 1024, 1024], P('fsdp', 'ctx'), may hold values from -6 to 6
Outputs:
- layer_output: bfloat16 [16, 1024, 1024], P('fsdp', 'ctx')
- input_gradient: bfloat16 [16, 1024, 1024], P('fsdp', 'ctx')
- gradient_joint_weight: float32 [1024, 3072], P('fsdp')
- gradient_joint_bias: float32 [2048], P('fsdp')
- gradient_mixer_weight: float32 [1024, 1024], P('fsdp')
- gradient_mixer_bias: float32 [1024], P('fsdp')
- gradient_first_gain: float32 [1024], P('fsdp')
- gradient_first_shift: float32 [1024], P('fsdp')
- gradient_expand_weight: float32 [1024, 4096], P('fsdp')
- gradient_expand_bias: float32 [4096], P('fsdp')
- gradient_shrink_weight: float32 [4096, 1024], P('fsdp')
- gradient_shrink_bias: float32 [1024], P('fsdp')
- gradient_second_gain: float32 [1024], P('fsdp')
- gradient_second_shift: float32 [1024], P('fsdp')
The draws below stay inside these ranges and needn't reach their ends.
Inputs may be any that keep to these rules, and one draw needn't show every extreme that they name: `segment_ids`: in each sequence the ids never fall, every id appears, and one document holds exactly 768 tokens.
All inputs are finite; a program needn't handle non-finite values.
Results may differ from the reference program's by a relative error of at most 0.04.
Values may be sent and summed in bfloat16 or wider, within the bound.
No kernel may reach another device: no remote copies, remote signals or barrier semaphores. Data moves between devices by JAX's collectives and lax.ppermute only.
A program may use at most 256 MiB of HBM per device.

```python
import math
import jax
import jax.numpy as jnp
import numpy as np
from jax import lax

D = 1024
HEADS = 16
HEAD = 64
FF = 4096
SEQ = 1024
DOCS = 4
SEQUENCES = 16


def spiked(entries, rng, source, target, parts, factor):
    owner, partner = [(jnp.arange(entries.shape[dim]) // (entries.shape[dim] // parts)).reshape([-1 if axis == dim else 1 for axis in range(entries.ndim)]) for dim in (source, target)]
    chosen = jax.random.permutation(rng, parts)[partner]
    strong = (owner == chosen) | (owner == (partner + parts // 2) % parts)
    return jnp.where(strong, factor * entries, entries)


def level_of(rng, dims, cuts, low, top_value):
    factor_of, own = 1.0, jax.random.fold_in(rng, 6)
    for dim, blocks in cuts:
        steps = jnp.exp(jax.random.uniform(jax.random.fold_in(own, dim), (blocks,), jnp.float32, low / len(cuts), top_value / len(cuts)))
        factor_of = factor_of * jnp.repeat(steps, dims[dim] // blocks).reshape([-1 if axis == dim else 1 for axis in range(len(dims))])
    return factor_of


def length_profile(amount, total, most, skew):
    loads = [(1 << 20) // math.isqrt(rank ** skew) + 1 for rank in range(2, amount + 1)]
    spare, holding = total - most - (amount - 1), [1] * (amount - 1)
    while spare > 0:
        free = [i for i in range(amount - 1) if holding[i] < most]
        mass, remaining = sum([loads[i] for i in free]), spare
        for i in free:
            more = min(most - holding[i], max(1, remaining * loads[i] // mass), spare)
            holding[i] = holding[i] + more
            spare = spare - more
    return np.array([most] + holding)


def ragged(key, amount, total, limit, skew):
    if amount == 2:
        one = jax.random.randint(key, (), max(1, total - limit), min(limit, total - 1) + 1)
        return jnp.stack([one, total - one])
    tallies = jnp.asarray(length_profile(amount, total, limit, skew), jnp.int32)
    couples = (amount - 1) // 2
    source_of, sink = tallies[1:1 + 2 * couples:2], tallies[2:2 + 2 * couples:2]
    room = jnp.minimum(source_of - 1, limit - sink)
    moved = jax.random.randint(jax.random.fold_in(key, 1), (couples,), 0, 1 << 20) % (room + 1)
    tallies = tallies.at[1:1 + 2 * couples:2].set(source_of - moved).at[2:2 + 2 * couples:2].set(sink + moved)
    return tallies[jax.random.permutation(jax.random.fold_in(key, 2), amount)]


def centred(rng, shape, deviation, reach, split=(), kind=jnp.bfloat16):
    drawn = jax.random.normal(rng, shape, jnp.float32) * deviation
    if len(split) > 0:
        drawn = level_of(rng, shape, split, -0.22, 0.18) * drawn
    return jnp.clip(drawn, min=-reach, max=reach).astype(kind)


def gaussian_with(stream_key, dims, width, reach, cuts, heavy, kind=jnp.bfloat16):
    entries = width * jax.random.normal(stream_key, dims, jnp.float32)
    if cuts:
        entries = entries * level_of(stream_key, dims, cuts, -0.22, 0.18)
    return jnp.clip(spiked(entries, jax.random.fold_in(stream_key, 3), *heavy), -reach, reach).astype(kind)


def setup_inputs(seed: int = 0) -> dict:
    streams_of = jax.random.split(jax.random.key(seed), 16)
    return {
        "hidden_in": gaussian_with(streams_of[0], (SEQUENCES, SEQ, D), 1.0, 6.0, ((0, 8), (1, 4)), (0, 2, 8, 2.0)),
        "segment_ids": jax.vmap(lambda own: jnp.searchsorted(jnp.cumsum(ragged(own, DOCS, SEQ, 3 * SEQ // 4, 0)), jnp.arange(SEQ), side="right"))(jax.random.split(streams_of[1], SEQUENCES)).reshape((SEQUENCES, SEQ)).astype(jnp.int32),
        "joint_weight": centred(streams_of[2], (D, 3 * D), D ** -0.5, 0.1875, ((0, 8),)),
        "joint_bias": centred(streams_of[3], (2 * D,), 0.5, 3.0, ((0, 8),)),
        "mixer_weight": centred(streams_of[4], (D, D), (D // 32) ** -0.5, 1.0, ((0, 8),)),
        "mixer_bias": centred(streams_of[5], (D,), 0.5, 3.0, ((0, 8),)),
        "first_gain": jnp.clip(1.0 + 0.1 * jax.random.normal(streams_of[6], (D,), jnp.float32), 0.5, 1.5).astype(jnp.bfloat16),
        "first_shift": centred(streams_of[7], (D,), 0.5, 3.0, ((0, 8),)),
        "expand_weight": centred(streams_of[8], (D, FF), D ** -0.5, 0.1875, ((0, 8),)),
        "expand_bias": centred(streams_of[9], (FF,), 0.5, 3.0, ((0, 8),)),
        "shrink_weight": centred(streams_of[10], (FF, D), FF ** -0.5, 0.09375, ((0, 8),)),
        "shrink_bias": centred(streams_of[11], (D,), 0.5, 3.0, ((0, 8),)),
        "second_gain": jnp.clip(1.0 + 0.1 * jax.random.normal(streams_of[12], (D,), jnp.float32), 0.5, 1.5).astype(jnp.bfloat16),
        "second_shift": centred(streams_of[13], (D,), 0.5, 3.0, ((0, 8),)),
        "output_cotangent": gaussian_with(streams_of[14], (SEQUENCES, SEQ, D), 1.0, 6.0, ((0, 8), (1, 4)), (0, 2, 8, 2.0)),
    }


@jax.custom_vjp
def low(v):
    return lax.optimization_barrier(v.astype(jnp.bfloat16)).astype(jnp.float32)

@jax.custom_vjp
def low_back(v):
    return v

def low_keep(v):
    return (low(v), None)

def low_pass(kept, grad):
    return (grad,)

def back_keep(v):
    return (v, None)

def back_low(kept, grad):
    return (low(grad),)
low.defvjp(low_keep, low_pass)
low_back.defvjp(back_keep, back_low)
NEG_FILL = -1e+30
EPSILON = 1e-12

def exact_dot(left, right):
    return jnp.dot(left, right, precision=lax.Precision.HIGHEST, preferred_element_type=jnp.float32)

def layer_norm(values, gain, shift):
    center = values - lax.optimization_barrier(jnp.mean(values, axis=-1, keepdims=True))
    factor = lax.rsqrt(lax.optimization_barrier(jnp.mean(center * center, axis=-1, keepdims=True)) + EPSILON)
    return center * factor * gain + shift

def gelu_exact(values):
    return jax.nn.gelu(values, approximate=False)

def layer_group(params, inputs, ids):
    joint, joint_offsets, mixer, mixer_offsets, gain_one, shift_one, expand, expand_offsets, shrink, shrink_offsets, gain_two, shift_two = params
    number = inputs.shape[0]
    flat = inputs.reshape(-1, D)
    offsets = jnp.concatenate([joint_offsets[:D], jnp.zeros((D,), jnp.float32), joint_offsets[D:]])
    projected = low(low_back(exact_dot(flat, joint) + offsets))
    queries = projected[:, :D].reshape(number, SEQ, HEADS, HEAD)
    keys = projected[:, D:2 * D].reshape(number, SEQ, HEADS, HEAD)
    values = projected[:, 2 * D:].reshape(number, SEQ, HEADS, HEAD)
    scores = jnp.einsum('sqhd,skhd->shqk', queries, keys, precision=lax.Precision.HIGHEST) * HEAD ** (-0.5)
    scores = low_back(scores)
    visible = ids[:, :, None] == ids[:, None, :]
    scores = jnp.where(visible[:, None], scores, NEG_FILL)
    weights = low(jax.nn.softmax(scores, axis=-1))
    mixed = jnp.einsum('shqk,skhd->sqhd', weights, values, precision=lax.Precision.HIGHEST)
    context = low(low_back(mixed.reshape(-1, D)))
    first_sum = flat + low_back(exact_dot(context, mixer) + mixer_offsets)
    normed = layer_norm(first_sum, gain_one, shift_one)
    lifted = low_back(exact_dot(low(normed), expand) + expand_offsets)
    active = low(gelu_exact(lifted))
    second_sum = normed + low_back(exact_dot(active, shrink) + shrink_offsets)
    return layer_norm(second_sum, gain_two, shift_two).reshape(number, SEQ, D)

def reference(hidden_in, segment_ids, joint_weight, joint_bias, mixer_weight, mixer_bias, first_gain, first_shift, expand_weight, expand_bias, shrink_weight, shrink_bias, second_gain, second_shift, output_cotangent):
    params = tuple((item.astype(jnp.float32) for item in (joint_weight, joint_bias, mixer_weight, mixer_bias, first_gain, first_shift, expand_weight, expand_bias, shrink_weight, shrink_bias, second_gain, second_shift)))
    inputs = hidden_in.astype(jnp.float32)
    group = math.gcd(SEQUENCES, 4)
    number = SEQUENCES // group
    ids = segment_ids.reshape(number, group, SEQ)
    stepper = jax.checkpoint(layer_group)

    def forward(inputs, params):
        shaped = inputs.reshape(number, group, SEQ, D)
        result = lax.map(lambda pair: stepper(params, pair[0], pair[1]), (shaped, ids))
        return result.reshape(SEQUENCES, SEQ, D)
    output, backward = jax.vjp(forward, inputs, params)
    input_grad, grads = backward(output_cotangent.astype(jnp.float32))
    return (output.astype(jnp.bfloat16), input_grad.astype(jnp.bfloat16), grads[0], grads[1], grads[2], grads[3], grads[4], grads[5], grads[6], grads[7], grads[8], grads[9], grads[10], grads[11])
```

```python
import functools

import jax
import jax.numpy as jnp
from jax import lax
from jax.experimental import pallas as pl
from jax.experimental.pallas import tpu as pltpu
from jax.sharding import PartitionSpec as P

HEAD = 64
NEG_FILL = -1e30
EPSILON = 1e-12
BF = jnp.bfloat16
F32 = jnp.float32
PAD = 16


def plain_dot(left, right):
    return jnp.dot(left, right, preferred_element_type=F32)


def left_dot(left, right):
    return lax.dot_general(left, right, (((0,), (0,)), ((), ())), preferred_element_type=F32)


def right_dot(left, right):
    return lax.dot_general(left, right, (((1,), (1,)), ((), ())), preferred_element_type=F32)


def norm_stats(values):
    center = values - jnp.mean(values, axis=-1, keepdims=True)
    factor = lax.rsqrt(jnp.mean(center * center, axis=-1, keepdims=True) + EPSILON)
    return center * factor, factor


def norm_back(grad, unit, factor, gain):
    scaled = grad * gain
    return factor * (
        scaled
        - jnp.mean(scaled, axis=-1, keepdims=True)
        - unit * jnp.mean(scaled * unit, axis=-1, keepdims=True)
    )


def gelu_exact(values):
    return jax.nn.gelu(values, approximate=False)


def mask_of(key_ids, query_ids):
    return jnp.where(key_ids == query_ids, 0.0, NEG_FILL).astype(F32)


def both(mine, other, lanes):
    return jnp.concatenate([mine[:, lanes], other[:, lanes]], axis=0)


def attend_kernel(q_ref, k_ref, v_ref, ko_ref, vo_ref, kid_ref, qid_ref, o_ref, lse_ref, bias):
    @pl.when(pl.program_id(0) == 0)
    def _():
        bias[...] = mask_of(kid_ref[...], qid_ref[...])

    outs = []
    for h in range(2):
        lanes = slice(h * HEAD, (h + 1) * HEAD)
        q = q_ref[:, lanes] * jnp.asarray(HEAD ** (-0.5), BF)
        k = both(k_ref, ko_ref, lanes)
        v = both(v_ref, vo_ref, lanes)
        scores = right_dot(k, q) + bias[...]
        top = jnp.max(scores, axis=0, keepdims=True)
        expo = jnp.exp(scores - top)
        total = jnp.sum(expo, axis=0, keepdims=True)
        outs.append(left_dot(v, expo.astype(BF)) / total)
        lse_ref[0, h : h + 1, :] = top + jnp.log(total)
    o_ref[...] = jnp.concatenate(outs, axis=0).T.astype(BF)


def attend_back_kernel(
    q_ref, k_ref, v_ref, ko_ref, vo_ref, kid_ref, qid_ref, do_ref, o_ref, lse_ref,
    dq_ref, mine_ref, other_ref, bias,
):
    @pl.when(pl.program_id(0) == 0)
    def _():
        bias[...] = mask_of(kid_ref[...], qid_ref[...])

    rows = q_ref.shape[0]
    scale = HEAD ** (-0.5)
    product = (do_ref[...].astype(F32) * o_ref[...].astype(F32)).T
    dqs, dks, dvs = [], [], []
    for h in range(2):
        lanes = slice(h * HEAD, (h + 1) * HEAD)
        q = q_ref[:, lanes] * jnp.asarray(scale, BF)
        k = both(k_ref, ko_ref, lanes)
        v = both(v_ref, vo_ref, lanes)
        do = do_ref[:, lanes]
        inner = jnp.sum(product[lanes, :], axis=0, keepdims=True)
        scores = right_dot(k, q) + bias[...]
        weights = jnp.exp(scores - lse_ref[0, h : h + 1, :])
        dvs.append(plain_dot(weights.astype(BF), do))
        weight_grad = right_dot(v, do)
        score_grad = (weights * (weight_grad - inner)).astype(BF)
        dks.append(plain_dot(score_grad, q))
        dqs.append(left_dot(k, score_grad) * scale)
    dq_ref[...] = jnp.concatenate(dqs, axis=0).T.astype(BF)
    dk = jnp.concatenate(dks, axis=1).astype(BF)
    dv = jnp.concatenate(dvs, axis=1).astype(BF)
    mine_ref[0] = dk[:rows]
    mine_ref[1] = dv[:rows]
    other_ref[0] = dk[rows:]
    other_ref[1] = dv[rows:]


def attention_specs(rows, pairs):
    def column(offset):
        return pl.BlockSpec((rows, 128), lambda h, offset=offset: (0, offset + h))

    ids = [
        pl.BlockSpec((2 * rows, 1), lambda h: (0, 0)),
        pl.BlockSpec((1, rows), lambda h: (0, 0)),
    ]
    return [column(0), column(pairs), column(2 * pairs), column(0), column(pairs)] + ids, column(0)


def attend(projected, received, key_ids, query_ids):
    rows, width = projected.shape[0], projected.shape[1] // 3
    pairs = width // 128
    specs, column = attention_specs(rows, pairs)
    stats = pl.BlockSpec((1, 2, rows), lambda h: (h, 0, 0))
    return pl.pallas_call(
        attend_kernel,
        grid=(pairs,),
        in_specs=specs,
        out_specs=[column, stats],
        out_shape=[
            jax.ShapeDtypeStruct((rows, width), BF),
            jax.ShapeDtypeStruct((pairs, 2, rows), F32),
        ],
        scratch_shapes=[pltpu.VMEM((2 * rows, rows), F32)],
        name="attend",
    )(projected, projected, projected, received, received, key_ids, query_ids)


def attend_back(projected, received, key_ids, query_ids, upstream, context, stats_in):
    rows, width = projected.shape[0], projected.shape[1] // 3
    pairs = width // 128
    specs, column = attention_specs(rows, pairs)
    stats = pl.BlockSpec((1, 2, rows), lambda h: (h, 0, 0))
    double = pl.BlockSpec((2, rows, 128), lambda h: (0, 0, h))
    return pl.pallas_call(
        attend_back_kernel,
        grid=(pairs,),
        in_specs=specs + [column, column, stats],
        out_specs=[column, double, double],
        out_shape=[
            jax.ShapeDtypeStruct((rows, width), BF),
            jax.ShapeDtypeStruct((2, rows, width), BF),
            jax.ShapeDtypeStruct((2, rows, width), BF),
        ],
        scratch_shapes=[pltpu.VMEM((2 * rows, rows), F32)],
        name="attend_back",
    )(projected, projected, projected, received, received, key_ids, query_ids, upstream, context, stats_in)


class Links:
    def __init__(self, shards, parts):
        self.shards, self.parts = shards, parts
        fsdp, ctx = lax.axis_index("fsdp"), lax.axis_index("ctx")
        self.side = fsdp % 2
        self.far, self.core = ctx // 2, ctx % 2
        self.lines = [list(range(s, shards, 2)) for s in range(2)]

    def swap_side(self, item):
        return lax.ppermute(item, "fsdp", [(i, i ^ 1) for i in range(self.shards)])

    def swap_far(self, item):
        return lax.ppermute(item, "ctx", [(i, i ^ 2) for i in range(self.parts)])

    def swap_core(self, item):
        return lax.ppermute(item, "ctx", [(i, i ^ 1) for i in range(self.parts)])


def pick(item, index, axis, parts=2):
    size = item.shape[axis] // parts
    return lax.dynamic_slice_in_dim(item, index * size, size, axis)


def ordered(index, mine, other, axis):
    first = jnp.where(index == 0, mine, other)
    second = jnp.where(index == 0, other, mine)
    return jnp.concatenate([first, second], axis=axis)


def gather_rows(links, part):
    line = lax.all_gather(part, "fsdp", axis=0, axis_index_groups=links.lines)
    other = links.swap_side(line)
    first = jnp.where(links.side == 0, line, other)
    second = jnp.where(links.side == 0, other, line)
    return jnp.stack([first, second], axis=1)


def gather_weight(links, shard):
    half = gather_rows(links, pick(shard, links.core, 1))
    lines, two, rows, cols = half.shape
    half = half.reshape(lines * two * rows, cols)
    return ordered(links.core, half, links.swap_core(half), 1)


def reduce_grad(links, keep, send):
    shards, rows, cols = keep.shape
    received = links.swap_core(send)

    def side_of(item, index):
        return lax.dynamic_slice_in_dim(item.reshape(shards // 2, 2, rows, cols), index, 1, 1)[:, 0]

    def total(index):
        return (side_of(keep, index).astype(F32) + side_of(received, index).astype(F32)).astype(BF)

    crossed = links.swap_side(total(1 - links.side))
    line = (total(links.side).astype(F32) + crossed.astype(F32)).astype(BF)
    return lax.psum_scatter(
        line, "fsdp", scatter_dimension=0, tiled=True, axis_index_groups=links.lines
    )[0]


def finish_grad(links, part):
    summed = part.astype(F32) + links.swap_far(part).astype(F32)
    return summed


def per_device(
    hidden_in,
    segment_ids,
    joint_weight,
    joint_bias,
    mixer_weight,
    mixer_bias,
    first_gain,
    first_shift,
    expand_weight,
    expand_bias,
    shrink_weight,
    shrink_bias,
    second_gain,
    second_shift,
    output_cotangent,
    *,
    shards,
    parts,
):
    seqs, local, width = hidden_in.shape
    rows = seqs * local
    links = Links(shards, parts)
    far, core, side = links.far, links.core, links.side

    def share(item):
        sent = lax.dynamic_slice_in_dim(item, 1 - far, 1, 0)[0]
        kept = lax.dynamic_slice_in_dim(item, far, 1, 0)[0]
        return jnp.concatenate([kept, links.swap_far(sent)], axis=0)

    def unshare(item):
        got = links.swap_far(item[local:])
        kept = item[:local]
        return jnp.where(far == 0, jnp.stack([kept, got]), jnp.stack([got, kept]))

    small = [joint_bias, mixer_bias, first_gain, first_shift, expand_bias, shrink_bias, second_gain, second_shift]
    sizes = [item.shape[0] for item in small]
    half_cols = joint_weight.shape[1] // 2
    count = sum(sizes)
    packed = jnp.pad(jnp.concatenate(small), (0, half_cols - count)).reshape(1, half_cols)
    packed = jnp.pad(packed, ((0, PAD - 1), (0, 0)))

    inputs = share(hidden_in)
    joint_part = jnp.concatenate([pick(joint_weight, core, 1), packed], axis=0)
    joint_half = gather_rows(links, joint_part)
    lines, _, tall, _ = joint_half.shape
    short = tall - PAD
    small_whole = joint_half[:, :, short, :count].reshape(shards, count)
    joint_half = joint_half[:, :, :short].reshape(shards * short, half_cols)
    joint_whole = ordered(core, joint_half, links.swap_core(joint_half), 1)
    vectors, at = [], 0
    for size in sizes:
        vectors.append(small_whole[:, at : at + size].reshape(shards * size).astype(F32))
        at += size
    joint_offsets, mixer_offsets, gain_one, shift_one, expand_offsets, shrink_offsets, gain_two, shift_two = vectors
    offsets = jnp.concatenate([joint_offsets[:width], jnp.zeros((width,), F32), joint_offsets[width:]])

    my_ids = lax.dynamic_slice_in_dim(segment_ids, far, 1, 0)[0]

    def id_block(index):
        return lax.dynamic_slice_in_dim(my_ids, index * local, local, 0)

    own_ids = [id_block(2 * far + core), id_block(2 * (1 - far) + core)]
    partner_ids = [id_block(2 * far + 1 - core), id_block(2 * (1 - far) + 1 - core)]
    query_ids = jnp.concatenate(own_ids).reshape(1, rows)
    key_ids = jnp.concatenate(own_ids + partner_ids).reshape(2 * rows, 1)

    projected = (plain_dot(inputs, joint_whole) + offsets).astype(BF)
    received = links.swap_core(projected[:, width:])
    mixer_whole = gather_weight(links, mixer_weight)
    context, stats = attend(projected, received, key_ids, query_ids)
    expand_whole = gather_weight(links, expand_weight)
    shrink_whole = gather_weight(links, shrink_weight)
    cotangent = share(output_cotangent).astype(F32)

    first_sum = inputs.astype(F32) + plain_dot(context, mixer_whole) + mixer_offsets
    unit_one, factor_one = norm_stats(first_sum)
    normed = unit_one * gain_one + shift_one
    normed_low = normed.astype(BF)
    lifted = plain_dot(normed_low, expand_whole) + expand_offsets
    active = gelu_exact(lifted).astype(BF)
    second_sum = normed + plain_dot(active, shrink_whole) + shrink_offsets
    unit_two, factor_two = norm_stats(second_sum)
    output = unshare((unit_two * gain_two + shift_two).astype(BF))

    second_grad = norm_back(cotangent, unit_two, factor_two, gain_two)
    gain_two_grad = jnp.sum(cotangent * unit_two, axis=0)
    shift_two_grad = jnp.sum(cotangent, axis=0)
    branch_low = second_grad.astype(BF)

    def weight_grad(left, right):
        def half(index):
            piece = left_dot(left, pick(right, index, 1)).astype(BF)
            return piece.reshape(shards, piece.shape[0] // shards, piece.shape[1])

        return half(core), half(1 - core)

    shrink_part = reduce_grad(links, *weight_grad(active, branch_low))
    shrink_offsets_grad = jnp.sum(branch_low, axis=0, dtype=F32)
    _, gelu_back = jax.vjp(gelu_exact, lifted)
    lifted_low = gelu_back(right_dot(branch_low, shrink_whole))[0].astype(BF)
    expand_part = reduce_grad(links, *weight_grad(normed_low, lifted_low))
    expand_offsets_grad = jnp.sum(lifted_low, axis=0, dtype=F32)
    normed_grad = second_grad + right_dot(lifted_low, expand_whole)

    first_grad = norm_back(normed_grad, unit_one, factor_one, gain_one)
    gain_one_grad = jnp.sum(normed_grad * unit_one, axis=0)
    shift_one_grad = jnp.sum(normed_grad, axis=0)
    branch_in = first_grad.astype(BF)
    mixer_part = reduce_grad(links, *weight_grad(context, branch_in))
    mixer_offsets_grad = jnp.sum(branch_in, axis=0, dtype=F32)
    context_grad = right_dot(branch_in, mixer_whole).astype(BF)
    query_grad, kept, given = attend_back(
        projected, received, key_ids, query_ids, context_grad, context, stats
    )
    both_grads = (kept.astype(F32) + links.swap_core(given).astype(F32)).astype(BF)
    joint_low = jnp.concatenate([query_grad, both_grads[0], both_grads[1]], axis=1)
    joint_offsets_grad = jnp.concatenate(
        [jnp.sum(query_grad, axis=0, dtype=F32), jnp.sum(both_grads[1], axis=0, dtype=F32)]
    )
    small_grads = [
        joint_offsets_grad, mixer_offsets_grad, gain_one_grad, shift_one_grad,
        expand_offsets_grad, shrink_offsets_grad, gain_two_grad, shift_two_grad,
    ]
    small_rows = jnp.concatenate([item.reshape(shards, -1) for item in small_grads], axis=1).astype(BF)
    small_rows = jnp.pad(small_rows[:, None], ((0, 0), (0, PAD - 1), (0, half_cols - count)))
    joint_keep, joint_send = weight_grad(inputs, joint_low)
    joint_part = reduce_grad(
        links,
        jnp.concatenate([joint_keep, small_rows], axis=1),
        jnp.concatenate([joint_send, small_rows], axis=1),
    )
    input_grad = unshare((first_grad + right_dot(joint_low, joint_whole)).astype(BF))

    def finish(part):
        summed = (part.astype(F32) + links.swap_far(part).astype(F32)).astype(BF)
        return summed

    def widen(summed):
        return ordered(core, summed, links.swap_core(summed), 1).astype(F32)

    joint_sum = finish(joint_part)
    small_sum = joint_sum[short, :count].astype(F32)
    results, at = [], 0
    for size in sizes:
        results.append(small_sum[at : at + size])
        at += size
    joint_bias_out, mixer_bias_out, gain_one_out, shift_one_out, expand_bias_out, shrink_bias_out, gain_two_out, shift_two_out = results
    return (
        output,
        input_grad,
        widen(joint_sum[:short]),
        joint_bias_out,
        widen(finish(mixer_part)),
        mixer_bias_out,
        gain_one_out,
        shift_one_out,
        widen(finish(expand_part)),
        expand_bias_out,
        widen(finish(shrink_part)),
        shrink_bias_out,
        gain_two_out,
        shift_two_out,
    )


def solution(mesh):
    whole = P("fsdp", "ctx", None)
    matrix, vector = P("fsdp", None), P("fsdp")
    return jax.shard_map(
        functools.partial(per_device, shards=mesh.shape["fsdp"], parts=mesh.shape["ctx"]),
        mesh=mesh,
        in_specs=(
            whole, matrix, matrix, vector, matrix, vector, vector, vector,
            matrix, vector, matrix, vector, vector, vector, whole,
        ),
        out_specs=(
            whole, whole, matrix, vector, matrix, vector, vector, vector,
            matrix, vector, matrix, vector, vector, vector,
        ),
        check_vma=False,
    )
```
